32 devices in a mesh: row: 4 (over y, core), col: 8 (over z, x).
Axes of the slice: x: 2, y: 2, z: 4, core: 2. Of those that a mesh axis runs over, the one named last changes fastest.
Arguments:
- a_vals: bfloat16 [256, 131072], P('row', 'col'), may hold values from -1.1953125 to 1.1953125
- p_vals: bfloat16 [64, 16384], P(None, ('row', 'col')), may hold values from -0.75 to 0.75
- a_rows: int32 [4, 2048], P('row', 'col'), may hold values from 0 to 63, as said below
- a_cols: int32 [4, 2048], P('row', 'col'), may hold values from 0 to 31, as said below
- a_count: int32 [4, 8], P('row', 'col'), may hold values from 64 to 256, as said below
- c_slot: int32 [4, 2048], P('row', 'col'), may hold values from 0 to 5, as said below
- agg: int32 [256], P(('row', 'col')), may hold values from 0 to 7, as said below
Outputs:
- coarse_vals: float32 [32, 24576], P(('row', 'col'))
The draws below stay inside these ranges and needn't reach their ends.
Inputs may be any that keep to these rules, and one draw needn't show every extreme that they name: Each tile's live slots are its first a_count ones; some tile of every row group has all 256 slots live. `agg`: in each row group, the aggregate numbers t*32//8 to (t+1)*32//8 - 1 are taken by the fine block rows of the row group's t-th column group of 32 rows, each number by exactly 8 of them. Coarse pattern: in row group r, slot k of coarse row a belongs to column group (a*6 + k + o_r) mod 8, for one shift o_r of the row group, and to one aggregate of that column group; every tile slot, live or not, has a fine row of aggregate a and a fine column of that slot's aggregate, with c_slot = k. The live slots of each tile reach every (a, k) pair of its column group. `a_rows`: see c_slot. `a_cols`: see c_slot.
All inputs are finite; a program needn't handle non-finite values.
Results may differ from the reference program's by a relative error of at most 0.0049.
Values may be sent and summed in bfloat16 or wider, within the bound.
A program may use at most 64 MiB of HBM per device.

```python
import jax
import jax.numpy as jnp
from jax import lax

BLOCK = 64
AGG = 8
KC = 6
NB = 256
RB = 64
CB = 32
KT = 256
CR = 8
NC = 32
N_ROW = 4
N_COL = 8


def draw_a_count(key, part):
    count_key, full_key = jax.random.split(key)
    counts = jax.random.randint(count_key, (N_ROW, N_COL), KT // 4, KT + 1)
    full_column = jax.random.randint(full_key, (N_ROW, 1), 0, N_COL)
    column_ids = jnp.arange(N_COL)[None, :]
    return jnp.where(column_ids == full_column, KT, counts).astype(jnp.int32)


def build_pattern(key):
    ratio = N_COL // N_ROW
    col_aggs = CB // AGG
    pairs = CR * KC // N_COL
    groups = jnp.arange(N_COL, dtype=jnp.int32)
    perm_key = jax.random.fold_in(key, 101)

    def one_perm(group):
        return jax.random.permutation(jax.random.fold_in(perm_key, group), CB).astype(jnp.int32)
    perms = jax.vmap(one_perm)(groups)
    inverse = jnp.argsort(perms, axis=1).astype(jnp.int32)
    agg_table = (groups[:, None] % ratio * col_aggs + inverse // AGG).reshape(NB).astype(jnp.int32)
    shifts = jax.random.randint(jax.random.fold_in(key, 102), (N_ROW,), 0, N_COL)
    col_choice = jax.random.randint(jax.random.fold_in(key, 103), (N_ROW, CR, KC), 0, col_aggs)
    shape = (N_ROW, N_COL, KT)
    slot_ids = jnp.arange(KT, dtype=jnp.int32)[None, None, :]
    chosen = jax.random.randint(jax.random.fold_in(key, 104), shape, 0, pairs)
    chosen = jnp.where(slot_ids < pairs, slot_ids, chosen)
    row_ids = jnp.broadcast_to(jnp.arange(N_ROW, dtype=jnp.int32)[:, None, None], shape)
    col_ids = jnp.broadcast_to(groups[None, :, None], shape)
    value = (col_ids - shifts[:, None, None]) % N_COL + chosen * N_COL
    coarse_row = value // KC
    slot_k = value % KC
    row_member = jax.random.randint(jax.random.fold_in(key, 105), shape, 0, AGG)
    owner_group = row_ids * ratio + coarse_row // col_aggs
    within = coarse_row % col_aggs * AGG + row_member
    rows = coarse_row // col_aggs * CB + perms[owner_group, within]
    target_agg = col_choice[row_ids, coarse_row, slot_k]
    col_member = jax.random.randint(jax.random.fold_in(key, 106), shape, 0, AGG)
    cols = perms[col_ids, target_agg * AGG + col_member]
    flat = (N_ROW, N_COL * KT)
    return (agg_table, rows.reshape(flat).astype(jnp.int32), cols.reshape(flat).astype(jnp.int32), slot_k.reshape(flat).astype(jnp.int32))


def draw_agg(key, part):
    return build_pattern(key)[0]


def draw_a_rows(key, part):
    return build_pattern(key)[1]


def draw_a_cols(key, part):
    return build_pattern(key)[2]


def draw_c_slot(key, part):
    return build_pattern(key)[3]


def block_levels(key, extent, pieces, least, largest):
    level, own = 1.0, jax.random.fold_in(key, 6)
    for dim, parts in pieces:
        draws = jnp.exp(jax.random.uniform(jax.random.fold_in(own, dim), (parts,), jnp.float32, least / len(pieces), largest / len(pieces)))
        level = level * jnp.repeat(draws, extent[dim] // parts).reshape([-1 if axis == dim else 1 for axis in range(len(extent))])
    return level


def bell_draw(own_key, extent, spread, limit, cuts=(), held_as=jnp.bfloat16):
    result = jax.random.normal(own_key, extent, jnp.float32) * spread
    if len(cuts) > 0:
        result = block_levels(own_key, extent, cuts, -0.22, 0.18) * result
    return jnp.clip(result, min=-limit, max=limit).astype(held_as)


def setup_inputs(seed: int = 0) -> dict:
    splits = jax.random.split(jax.random.key(seed), 8)
    a_vals = bell_draw(splits[0], (N_ROW * BLOCK, N_COL * KT * BLOCK), 0.2, 1.1953125, ((0, 4), (1, 8)))
    p_vals = bell_draw(splits[1], (BLOCK, NB * BLOCK), BLOCK ** -0.5, 0.75, ((1, 32),))
    a_rows = draw_a_rows(jax.random.fold_in(splits[7], 71), 0)
    a_cols = draw_a_cols(jax.random.fold_in(splits[7], 71), 0)
    a_count = draw_a_count(jax.random.fold_in(splits[7], 71), 0)
    c_slot = draw_c_slot(jax.random.fold_in(splits[7], 71), 0)
    agg = draw_agg(jax.random.fold_in(splits[7], 71), 0)
    return dict(a_vals=a_vals, p_vals=p_vals, a_rows=a_rows, a_cols=a_cols, a_count=a_count, c_slot=c_slot, agg=agg)


def reference(a_vals, p_vals, a_rows, a_cols, a_count, c_slot, agg):
    prolong = p_vals.reshape(BLOCK, NB, BLOCK)
    blocks_all = a_vals.reshape(N_ROW, BLOCK, N_COL, KT, BLOCK)
    segments = CR * KC

    def row_group(group_index):
        row_panel = lax.dynamic_slice_in_dim(prolong, group_index * RB, RB, 1)
        group_agg = lax.dynamic_slice_in_dim(agg, group_index * RB, RB, 0)
        group_blocks = lax.dynamic_index_in_dim(blocks_all, group_index, 0, False)
        group_rows = lax.dynamic_index_in_dim(a_rows, group_index, 0, False).reshape(N_COL, KT)
        group_cols = lax.dynamic_index_in_dim(a_cols, group_index, 0, False).reshape(N_COL, KT)
        group_slots = lax.dynamic_index_in_dim(c_slot, group_index, 0, False).reshape(N_COL, KT)
        group_counts = lax.dynamic_index_in_dim(a_count, group_index, 0, False)

        def tile(running, tile_index):
            tile_blocks = lax.dynamic_index_in_dim(group_blocks, tile_index, 1, False)
            col_panel = lax.dynamic_slice_in_dim(prolong, tile_index * CB, CB, 1)
            slot_rows = lax.dynamic_index_in_dim(group_rows, tile_index, 0, False)
            slot_cols = lax.dynamic_index_in_dim(group_cols, tile_index, 0, False)
            coarse_slot = lax.dynamic_index_in_dim(group_slots, tile_index, 0, False)
            live_count = lax.dynamic_index_in_dim(group_counts, tile_index, 0, False)
            left = jnp.take(row_panel, slot_rows, axis=1).astype(jnp.float32)
            half = jnp.einsum('fsa,fsj->saj', left, tile_blocks.astype(jnp.float32)).astype(jnp.bfloat16)
            right = jnp.take(col_panel, slot_cols, axis=1).astype(jnp.float32)
            triple = jnp.einsum('saj,jsb->sab', half.astype(jnp.float32), right).astype(jnp.bfloat16)
            live_mask = jnp.arange(KT, dtype=jnp.int32) < live_count
            target = jnp.where(live_mask, jnp.take(group_agg, slot_rows) * KC + coarse_slot, segments).astype(jnp.int32)
            summed = jax.ops.segment_sum(triple.reshape(KT, BLOCK * BLOCK).astype(jnp.float32), target, num_segments=segments + 1)[:segments]
            rounded = lax.optimization_barrier(summed.reshape(CR, KC * BLOCK * BLOCK).astype(jnp.bfloat16))
            return running + rounded.astype(jnp.float32), None

        start_value = jnp.zeros((CR, KC * BLOCK * BLOCK), jnp.float32)
        total, _ = lax.scan(tile, start_value, jnp.arange(N_COL, dtype=jnp.int32))
        return total

    return lax.map(row_group, jnp.arange(N_ROW, dtype=jnp.int32)).reshape(NC, KC * BLOCK * BLOCK)
```

```python
import functools

import jax
import jax.numpy as jnp
from jax import lax
from jax.experimental import pallas as pl
from jax.experimental.pallas import tpu as pltpu
from jax.sharding import PartitionSpec as P

AGG = 8
KC = 6
LO = 2
UNROLL = 8
MESH = pl.DeviceIdType.MESH
F32 = jnp.float32
BF16 = jnp.bfloat16


def kernel(
    n_row, n_col, pk_ref, idx_ref, k0_ref, a_hbm, p_ref, ag_ref, out_ref,
    a_v, pan, agp, colp, pz, ps, q_ref, snd, rcv,
    a_sem, p_send, p_recv, g_send, g_recv, c_send, c_recv, x_send, x_recv,
):
    bw = p_ref.shape[0]
    dev_rows = ag_ref.shape[0]
    slots = ps.shape[0] - 1
    ratio = n_col // n_row
    per = n_col // ratio
    owners = per * dev_rows // AGG
    hi = n_col // LO
    row = lax.axis_index("row")
    me = lax.axis_index("col")
    z, x = me // LO, lax.rem(me, LO)
    is_root = row == me // ratio
    part = lax.rem(me, ratio)

    @pl.loop(0, slots // 2)
    def _(i):
        lanes = pl.ds(pl.multiple_of(i * (2 * bw), 2 * bw), 2 * bw)
        pltpu.make_async_copy(a_hbm.at[:, lanes], a_v.at[i], a_sem).start()

    def col_of(d):
        return lax.rem(me + d, n_col)

    barrier = pltpu.get_barrier_semaphore()
    for d in range(1, n_col):
        pl.semaphore_signal(barrier, inc=1, device_id=(row, col_of(d)), device_id_type=MESH)
    for d in range(1, n_row):
        pl.semaphore_signal(
            barrier, inc=1, device_id=(lax.rem(row + d, n_row), me), device_id_type=MESH
        )
    pan[me] = p_ref[...]
    agp[me] = ag_ref[...]
    pl.semaphore_wait(barrier, n_col + n_row - 2)

    def remote(src, dst, s, r, dev):
        return pltpu.make_async_remote_copy(
            src_ref=src, dst_ref=dst, send_sem=s, recv_sem=r, device_id=dev, device_id_type=MESH
        )

    own = []
    for d in range(1, hi):
        to = lax.rem(z + d, hi) * LO + x
        own.append(remote(p_ref, pan.at[me], p_send.at[len(own)], p_recv.at[me], (row, to)))
    partner = z * LO + (1 - x)
    own.append(remote(p_ref, pan.at[me], p_send.at[len(own)], p_recv.at[me], (row, partner)))
    for c in own:
        c.start()

    def panel_copies(q, src):
        m = lax.rem(q, per)
        return [
            remote(
                src, colp.at[m], c_send.at[m, d - 1], c_recv.at[m],
                (lax.rem(row + d, n_row), me),
            )
            for d in range(1, n_row)
        ]

    def hand_on(q, src):
        @pl.when(is_root & (q // per == part))
        def _():
            for c in panel_copies(q, src):
                c.start()

    hand_on(me, p_ref)
    marks = [
        remote(ag_ref, agp.at[me], g_send.at[d - 1], g_recv.at[me], (row, col_of(d)))
        for d in range(1, n_col)
    ]
    for c in marks:
        c.start()

    pz[...] = jnp.zeros_like(pz)
    ps[slots] = jnp.zeros((bw, bw), BF16)
    q_ref[...] = jnp.zeros_like(q_ref)

    def landed(q):
        remote(p_ref, pan.at[q], p_send.at[0], p_recv.at[q], (row, partner)).wait_recv()

    passed = []
    landed(partner)
    hand_on(partner, pan.at[partner])
    for d in range(1, hi):
        q = lax.rem(z + hi - d, hi) * LO + x
        landed(q)
        c = remote(
            pan.at[q], pan.at[q], p_send.at[hi - 1 + d], p_recv.at[q], (row, partner)
        )
        c.start()
        passed.append(c)
        hand_on(q, pan.at[q])
    for d in range(1, hi):
        q = lax.rem(z + hi - d, hi) * LO + (1 - x)
        landed(q)
        hand_on(q, pan.at[q])

    for m in range(per):
        @pl.when(is_root)
        def _():
            colp[m] = pan[part * per + m]

        @pl.when(jnp.logical_not(is_root))
        def _():
            remote(
                p_ref, colp.at[m], c_send.at[m, 0], c_recv.at[m], (row, partner)
            ).wait_recv()

        for b in range(dev_rows):
            block = colp[m, :, b * bw:(b + 1) * bw]
            pz[2 * (m * dev_rows + b), 0:bw, :] = block
            pz[2 * (m * dev_rows + b) + 1, bw:2 * bw, :] = block
    pltpu.make_async_copy(a_v, a_v, a_sem).wait()

    def steps(it, acc):
        for u in range(UNROLL):
            at = it * UNROLL + u
            left = a_v[pk_ref[0, at]]
            right = pz[pk_ref[1, at]]
            keep = pk_ref[2, at].astype(F32)
            prod = jnp.dot(left, right, preferred_element_type=F32)
            acc = acc * keep + prod
            ps[at] = acc.astype(BF16)
        return acc

    lax.fori_loop(0, slots // UNROLL, steps, jnp.zeros((bw, bw), F32))

    for d in range(1, n_col):
        q = col_of(d)
        remote(ag_ref, agp.at[q], g_send.at[0], g_recv.at[q], (row, partner)).wait_recv()

    lane = lax.broadcasted_iota(jnp.int32, (1, 2 * bw), 1)

    def fold(c, carry):
        group = c // per
        base = (group * owners).astype(F32)
        total = jnp.zeros((owners * bw, bw), F32)
        for h in range(dev_rows // 4):
            wide = []
            for e in range(2):
                b = 4 * h + 2 * e
                flip = pan[c, :, b * bw:(b + 2) * bw].T
                pair = jnp.concatenate([flip[:bw], flip[bw:]], axis=1)
                mark = jnp.where(lane < bw, agp[c, b:b + 1, :], agp[c, b + 1:b + 2, :]) - base
                wide.append(
                    jnp.concatenate(
                        [pair * jnp.where(mark == o, 1.0, 0.0).astype(BF16) for o in range(owners)],
                        axis=0,
                    )
                )
            right = jnp.concatenate(
                [ps[idx_ref[0, c * dev_rows + 4 * h + e]] for e in range(4)], axis=0
            )
            total += jnp.dot(
                jnp.concatenate(wide, axis=1), right, preferred_element_type=F32
            )
        q_ref[group] += total
        return carry

    lax.fori_loop(0, n_col, fold, 0)

    half = bw // 2
    for o in range(n_col):
        g, w = o // owners, o % owners
        even = q_ref[g, pl.ds(w * bw, half, stride=2), :]
        odd = q_ref[g, pl.ds(w * bw + 1, half, stride=2), :]
        snd[o] = jnp.concatenate([even, odd], axis=1).astype(BF16)
    terms = []
    for d in range(1, n_col):
        to = col_of(d)
        terms.append(remote(snd.at[to], rcv.at[me], x_send.at[d - 1], x_recv.at[me], (row, to)))
    for c in terms:
        c.start()
    rcv[me] = snd[me]

    there = lax.broadcasted_iota(jnp.int32, (dev_rows, 2 * bw), 0) == k0_ref[0, 1]
    spot = jnp.sum(jnp.where(there, agp[k0_ref[0, 0]], 0.0), axis=0, keepdims=True)
    spot = spot.astype(jnp.int32) * KC + k0_ref[0, 2]
    for d in range(1, n_col):
        q = col_of(d)
        remote(snd.at[0], rcv.at[q], x_send.at[0], x_recv.at[q], (row, partner)).wait_recv()
    sums = [jnp.zeros((half, 2 * bw), F32) for _ in range(KC)]
    for c in range(n_col):
        value = rcv[c].astype(F32)
        where = (spot + (c - (KC + 1) * me + 8 * n_col * n_col)) & (n_col - 1)
        for k in range(KC):
            sums[k] += jnp.where(where == k, value, 0.0)
    for k in range(KC):
        out_ref[k * half:(k + 1) * half, :] = sums[k]

    for c in own + passed + marks + terms:
        c.wait_send()
    for m in range(per):
        @pl.when(is_root)
        def _():
            for c in panel_copies(m, pan.at[0]):
                c.wait_send()


def on_device(n_row, n_col, a_vals, p_vals, a_rows, a_cols, a_count, c_slot, agg):
    bw = p_vals.shape[0]
    dev_rows = agg.shape[0]
    slots = a_rows.shape[1]
    rows_group = dev_rows * n_col
    ratio = n_col // n_row
    cols_group = rows_group // ratio
    per = n_col // ratio
    assert rows_group // AGG == n_col and n_col & (n_col - 1) == 0 and n_col >= KC
    cb = (cols_group - 1).bit_length()
    sb = (slots - 1).bit_length()
    ids = jnp.arange(slots, dtype=jnp.int32)
    key = jnp.where(ids < a_count[0, 0], a_rows[0], rows_group)
    word = (((key << sb) | ids) << cb) | a_cols[0]
    rank = jnp.sum((word[None, :] < word[:, None]).astype(jnp.int32), axis=1)
    packed = jnp.sum(jnp.where(rank[None, :] == ids[:, None], word[None, :], 0), axis=1)
    tops = packed >> (cb + sb)
    keep = jnp.concatenate([jnp.zeros((1,), jnp.int32), (tops[1:] == tops[:-1]).astype(jnp.int32)])
    slot = (packed >> cb) & ((1 << sb) - 1)
    col = packed & ((1 << cb) - 1)
    plan = jnp.stack([slot >> 1, 2 * col + (slot & 1), keep])
    rows = jnp.arange(rows_group, dtype=jnp.int32)
    upto = jnp.sum((key[None, :] <= rows[:, None]).astype(jnp.int32), axis=1)
    seen = jnp.any(key[None, :] == rows[:, None], axis=1)
    last = jnp.where(seen, upto - 1, slots)
    lead = jnp.stack([a_rows[0, 0] // dev_rows, a_rows[0, 0] % dev_rows, c_slot[0, 0]])[None]
    marks = jnp.broadcast_to(agg.astype(F32)[:, None], (dev_rows, 2 * bw))
    smem = pl.BlockSpec(memory_space=pltpu.SMEM)
    vmem = pl.BlockSpec(memory_space=pltpu.VMEM)
    dma = pltpu.SemaphoreType.DMA
    owners = per * dev_rows // AGG
    out = pl.pallas_call(
        functools.partial(kernel, n_row, n_col),
        out_shape=jax.ShapeDtypeStruct((KC * bw // 2, 2 * bw), F32),
        in_specs=[smem, smem, smem, pl.BlockSpec(memory_space=pl.ANY), vmem, vmem],
        out_specs=vmem,
        scratch_shapes=[
            pltpu.VMEM((slots // 2, bw, 2 * bw), BF16),
            pltpu.VMEM((n_col, bw, dev_rows * bw), BF16),
            pltpu.VMEM((n_col, dev_rows, 2 * bw), F32),
            pltpu.VMEM((per, bw, dev_rows * bw), BF16),
            pltpu.VMEM((2 * cols_group, 2 * bw, bw), BF16),
            pltpu.VMEM((slots + 1, bw, bw), BF16),
            pltpu.VMEM((ratio, owners * bw, bw), F32),
            pltpu.VMEM((n_col, bw // 2, 2 * bw), BF16),
            pltpu.VMEM((n_col, bw // 2, 2 * bw), BF16),
            dma,
            dma((n_col,)), dma((n_col,)),
            dma((n_col,)), dma((n_col,)),
            dma((per, n_row)), dma((per,)),
            dma((n_col,)), dma((n_col,)),
        ],
        compiler_params=pltpu.CompilerParams(
            collective_id=0, has_side_effects=True, vmem_limit_bytes=48 << 20
        ),
    )(plan, last.reshape(1, rows_group), lead, a_vals, p_vals, marks)
    return out.reshape(1, KC * bw * bw)


def solution(mesh):
    return jax.shard_map(
        functools.partial(on_device, mesh.shape["row"], mesh.shape["col"]),
        mesh=mesh,
        in_specs=(
            P("row", "col"),
            P(None, ("row", "col")),
            P("row", "col"),
            P("row", "col"),
            P("row", "col"),
            P("row", "col"),
            P(("row", "col")),
        ),
        out_specs=P(("row", "col"), None),
        check_vma=False,
    )
```

```python
import functools

import jax
import jax.numpy as jnp
from jax import lax
from jax.experimental import pallas as pl
from jax.experimental.pallas import tpu as pltpu
from jax.sharding import PartitionSpec as P

AGG = 8
KC = 6
LO = 2
UNROLL = 8
MESH = pl.DeviceIdType.MESH
F32 = jnp.float32
BF16 = jnp.bfloat16


def within(at, size):
    return jnp.minimum(jnp.maximum(at, 0), size - 1)


def make_plan(rows_group, cols_group, dev_rows, small, count_v, plan_v):
    slots, width = small.shape[2], plan_v.shape[1]
    cb, sb, db = (n.bit_length() - 1 for n in (cols_group, slots, dev_rows))
    rows, cols = small[0], small[1]
    lane = lax.broadcasted_iota(jnp.int32, (1, slots), 1)
    key = jnp.where(lane < count_v[...], rows, rows_group)
    across = jnp.broadcast_to(((((key << sb) | lane) << cb) | cols), (slots, slots))
    side = lax.broadcasted_iota(jnp.int32, (slots, slots), 0)
    place = lax.broadcasted_iota(jnp.int32, (slots, slots), 1)
    down = jnp.sum(jnp.where(side == place, across, 0), axis=1, keepdims=True)
    rank = jnp.sum(jnp.where(across < down, 1, 0), axis=1, keepdims=True)
    word = jnp.sum(jnp.where(rank == place, down, 0), axis=0, keepdims=True)
    slot = (word >> cb) & (slots - 1)
    top = word >> (cb + sb)
    same = (top == pltpu.roll(top, 1, 1)) & (lane > 0)
    target = lax.broadcasted_iota(jnp.int32, (slots, width), 1)
    tops = down >> (cb + sb)
    upto = jnp.sum(jnp.where(tops <= target, 1, 0), axis=0, keepdims=True)
    before = jnp.sum(jnp.where(tops < target, 1, 0), axis=0, keepdims=True)
    last = jnp.where(upto > before, upto - 1, slots)
    plan_v[...] = jnp.zeros_like(plan_v)
    plan_v[0:1, :slots] = slot >> 1
    plan_v[1:2, :slots] = 2 * (word & (cols_group - 1)) + (slot & 1)
    plan_v[2:3, :slots] = same.astype(jnp.int32)
    plan_v[3:4, :] = last
    plan_v[4:5, :slots] = rows >> db
    plan_v[5:6, :slots] = rows & (dev_rows - 1)
    plan_v[6:7, :slots] = small[2]


def kernel(
    n_row, n_col, a_hbm, p_hbm, rows_hbm, cols_hbm, count_hbm, kslot_hbm, agg_hbm, out_ref,
    small, count_v, agg_v, plan_v, plan_s, ag_ref, in_sem, plan_sem, a_v, pan, agp, colp, pz, ps, q_ref, snd, rcv,
    a_sem, p_send, p_recv, g_send, g_recv, c_send, c_recv, x_send, x_recv,
):
    bw = p_hbm.shape[0]
    dev_rows = ag_ref.shape[0]
    rows_group = n_col * dev_rows
    slots = ps.shape[0] - 1
    ratio = n_col // n_row
    per = n_col // ratio
    owners = per * dev_rows // AGG
    hi = n_col // LO
    row = lax.axis_index("row")
    me = lax.axis_index("col")
    z, x = me // LO, lax.rem(me, LO)
    is_root = row == me // ratio
    part = lax.rem(me, ratio)

    p_ref = pan.at[me]
    loads = [
        pltpu.make_async_copy(src, dst, in_sem.at[i])
        for i, (src, dst) in enumerate(
            [
                (p_hbm, p_ref),
                (rows_hbm, small.at[0]),
                (cols_hbm, small.at[1]),
                (kslot_hbm, small.at[2]),
                (count_hbm, count_v),
                (agg_hbm, agg_v),
            ]
        )
    ]
    for c in loads:
        c.start()

    @pl.loop(0, slots // 2)
    def _(i):
        lanes = pl.ds(pl.multiple_of(i * (2 * bw), 2 * bw), 2 * bw)
        pltpu.make_async_copy(a_hbm.at[:, lanes], a_v.at[i], a_sem).start()

    def col_of(d):
        return lax.rem(me + d, n_col)

    barrier = pltpu.get_barrier_semaphore()
    for d in range(1, n_col):
        pl.semaphore_signal(barrier, inc=1, device_id=(row, col_of(d)), device_id_type=MESH)
    for d in range(1, n_row):
        pl.semaphore_signal(
            barrier, inc=1, device_id=(lax.rem(row + d, n_row), me), device_id_type=MESH
        )
    for c in loads:
        c.wait()
    square = (dev_rows, dev_rows)
    eye = lax.broadcasted_iota(jnp.int32, square, 0) == lax.broadcasted_iota(jnp.int32, square, 1)
    mine = jnp.where(eye, jnp.broadcast_to(agg_v[...].astype(F32), square), 0.0)
    mine = jnp.broadcast_to(jnp.sum(mine, axis=1, keepdims=True), ag_ref.shape)
    ag_ref[...] = mine
    agp[me] = mine
    make_plan(rows_group, n_col // (n_col // n_row) * dev_rows, dev_rows, small, count_v, plan_v)
    pl.semaphore_wait(barrier, n_col + n_row - 2)

    def remote(src, dst, s, r, dev):
        return pltpu.make_async_remote_copy(
            src_ref=src, dst_ref=dst, send_sem=s, recv_sem=r, device_id=dev, device_id_type=MESH
        )

    own = []
    for d in range(1, hi):
        to = lax.rem(z + d, hi) * LO + x
        own.append(remote(p_ref, pan.at[me], p_send.at[len(own)], p_recv.at[me], (row, to)))
    partner = z * LO + (1 - x)
    own.append(remote(p_ref, pan.at[me], p_send.at[len(own)], p_recv.at[me], (row, partner)))
    for c in own:
        c.start()

    def panel_copies(q, src):
        m = lax.rem(q, per)
        return [
            remote(
                src, colp.at[m], c_send.at[m, d - 1], c_recv.at[m],
                (lax.rem(row + d, n_row), me),
            )
            for d in range(1, n_row)
        ]

    def hand_on(q, src):
        @pl.when(is_root & (q // per == part))
        def _():
            for c in panel_copies(q, src):
                c.start()

    plan_copy = pltpu.make_async_copy(plan_v, plan_s, plan_sem)
    plan_copy.start()
    hand_on(me, p_ref)
    marks = [
        remote(ag_ref, agp.at[me], g_send.at[d - 1], g_recv.at[me], (row, col_of(d)))
        for d in range(1, n_col)
    ]
    for c in marks:
        c.start()

    pz[...] = jnp.zeros_like(pz)
    ps[slots] = jnp.zeros((bw, bw), BF16)
    q_ref[...] = jnp.zeros_like(q_ref)

    def landed(q):
        remote(p_ref, pan.at[q], p_send.at[0], p_recv.at[q], (row, partner)).wait_recv()

    passed = []
    landed(partner)
    hand_on(partner, pan.at[partner])
    for d in range(1, hi):
        q = lax.rem(z + hi - d, hi) * LO + x
        landed(q)
        c = remote(
            pan.at[q], pan.at[q], p_send.at[hi - 1 + d], p_recv.at[q], (row, partner)
        )
        c.start()
        passed.append(c)
        hand_on(q, pan.at[q])
    for d in range(1, hi):
        q = lax.rem(z + hi - d, hi) * LO + (1 - x)
        landed(q)
        hand_on(q, pan.at[q])

    for m in range(per):
        @pl.when(is_root)
        def _():
            colp[m] = pan[part * per + m]

        @pl.when(jnp.logical_not(is_root))
        def _():
            remote(
                p_ref, colp.at[m], c_send.at[m, 0], c_recv.at[m], (row, partner)
            ).wait_recv()

        for b in range(dev_rows):
            block = colp[m, :, b * bw:(b + 1) * bw]
            pz[2 * (m * dev_rows + b), 0:bw, :] = block
            pz[2 * (m * dev_rows + b) + 1, bw:2 * bw, :] = block
    pltpu.make_async_copy(a_v, a_v, a_sem).wait()

    plan_copy.wait()

    def steps(it, acc):
        for u in range(UNROLL):
            at = it * UNROLL + u
            left = a_v[within(plan_s[0, at], slots // 2)]
            right = pz[within(plan_s[1, at], pz.shape[0])]
            keep = plan_s[2, at].astype(F32)
            prod = jnp.dot(left, right, preferred_element_type=F32)
            acc = acc * keep + prod
            ps[at] = acc.astype(BF16)
        return acc

    lax.fori_loop(0, slots // UNROLL, steps, jnp.zeros((bw, bw), F32))

    for d in range(1, n_col):
        q = col_of(d)
        remote(ag_ref, agp.at[q], g_send.at[0], g_recv.at[q], (row, partner)).wait_recv()

    lane = lax.broadcasted_iota(jnp.int32, (1, 2 * bw), 1)

    def fold(c, carry):
        group = c // per
        base = (group * owners).astype(F32)
        total = jnp.zeros((owners * bw, bw), F32)
        for h in range(dev_rows // 4):
            wide = []
            for e in range(2):
                b = 4 * h + 2 * e
                flip = pan[c, :, b * bw:(b + 2) * bw].T
                pair = jnp.concatenate([flip[:bw], flip[bw:]], axis=1)
                mark = jnp.where(lane < bw, agp[c, b:b + 1, :], agp[c, b + 1:b + 2, :]) - base
                wide.append(
                    jnp.concatenate(
                        [pair * jnp.where(mark == o, 1.0, 0.0).astype(BF16) for o in range(owners)],
                        axis=0,
                    )
                )
            right = jnp.concatenate(
                [ps[within(plan_s[3, c * dev_rows + 4 * h + e], slots + 1)] for e in range(4)], axis=0
            )
            total += jnp.dot(
                jnp.concatenate(wide, axis=1), right, preferred_element_type=F32
            )
        q_ref[group] += total
        return carry

    lax.fori_loop(0, n_col, fold, 0)

    half = bw // 2
    for o in range(n_col):
        g, w = o // owners, o % owners
        even = q_ref[g, pl.ds(w * bw, half, stride=2), :]
        odd = q_ref[g, pl.ds(w * bw + 1, half, stride=2), :]
        snd[o] = jnp.concatenate([even, odd], axis=1).astype(BF16)
    terms = []
    for d in range(1, n_col):
        to = col_of(d)
        terms.append(remote(snd.at[to], rcv.at[me], x_send.at[d - 1], x_recv.at[me], (row, to)))
    for c in terms:
        c.start()
    rcv[me] = snd[me]

    there = lax.broadcasted_iota(jnp.int32, (dev_rows, 2 * bw), 0) == plan_s[5, 0]
    spot = jnp.sum(jnp.where(there, agp[within(plan_s[4, 0], n_col)], 0.0), axis=0, keepdims=True)
    spot = spot.astype(jnp.int32) * KC + plan_s[6, 0]
    for d in range(1, n_col):
        q = col_of(d)
        remote(snd.at[0], rcv.at[q], x_send.at[0], x_recv.at[q], (row, partner)).wait_recv()
    sums = [jnp.zeros((half, 2 * bw), F32) for _ in range(KC)]
    for c in range(n_col):
        value = rcv[c].astype(F32)
        where = (spot + (c - (KC + 1) * me + 8 * n_col * n_col)) & (n_col - 1)
        for k in range(KC):
            sums[k] += jnp.where(where == k, value, 0.0)
    for k in range(KC):
        out_ref[k * half:(k + 1) * half, :] = sums[k]

    for c in own + passed + marks + terms:
        c.wait_send()
    for m in range(per):
        @pl.when(is_root)
        def _():
            for c in panel_copies(m, pan.at[0]):
                c.wait_send()


def on_device(n_row, n_col, a_vals, p_vals, a_rows, a_cols, a_count, c_slot, agg):
    bw = p_vals.shape[0]
    dev_rows = agg.shape[0]
    slots = a_rows.shape[1]
    rows_group = dev_rows * n_col
    ratio = n_col // n_row
    cols_group = rows_group // ratio
    per = n_col // ratio
    assert rows_group // AGG == n_col and n_col >= KC
    assert all(n & (n - 1) == 0 for n in (n_col, slots, cols_group, dev_rows))
    keep = pl.BlockSpec(memory_space=pltpu.HBM)
    vmem = pl.BlockSpec(memory_space=pltpu.VMEM)
    dma = pltpu.SemaphoreType.DMA
    owners = per * dev_rows // AGG
    out = pl.pallas_call(
        functools.partial(kernel, n_row, n_col),
        out_shape=jax.ShapeDtypeStruct((KC * bw // 2, 2 * bw), F32),
        in_specs=[keep] * 7,
        out_specs=vmem,
        scratch_shapes=[
            pltpu.VMEM((3, 1, slots), jnp.int32),
            pltpu.VMEM((1, 1), jnp.int32),
            pltpu.VMEM((1, dev_rows), jnp.int32),
            pltpu.VMEM((8, max(slots, rows_group)), jnp.int32),
            pltpu.SMEM((8, max(slots, rows_group)), jnp.int32),
            pltpu.VMEM((dev_rows, 2 * bw), F32),
            dma((6,)), dma,
            pltpu.VMEM((slots // 2, bw, 2 * bw), BF16),
            pltpu.VMEM((n_col, bw, dev_rows * bw), BF16),
            pltpu.VMEM((n_col, dev_rows, 2 * bw), F32),
            pltpu.VMEM((per, bw, dev_rows * bw), BF16),
            pltpu.VMEM((2 * cols_group, 2 * bw, bw), BF16),
            pltpu.VMEM((slots + 1, bw, bw), BF16),
            pltpu.VMEM((ratio, owners * bw, bw), F32),
            pltpu.VMEM((n_col, bw // 2, 2 * bw), BF16),
            pltpu.VMEM((n_col, bw // 2, 2 * bw), BF16),
            dma,
            dma((n_col,)), dma((n_col,)),
            dma((n_col,)), dma((n_col,)),
            dma((per, n_row)), dma((per,)),
            dma((n_col,)), dma((n_col,)),
        ],
        compiler_params=pltpu.CompilerParams(
            collective_id=0, has_side_effects=True, vmem_limit_bytes=67043328
        ),
    )(a_vals, p_vals, a_rows, a_cols, a_count, c_slot, agg.reshape(1, dev_rows))
    return out.reshape(1, KC * bw * bw)


def solution(mesh):
    return jax.shard_map(
        functools.partial(on_device, mesh.shape["row"], mesh.shape["col"]),
        mesh=mesh,
        in_specs=(
            P("row", "col"),
            P(None, ("row", "col")),
            P("row", "col"),
            P("row", "col"),
            P("row", "col"),
            P("row", "col"),
            P(("row", "col")),
        ),
        out_specs=P(("row", "col"), None),
        check_vma=False,
    )
```

```python
import functools

import jax
import jax.numpy as jnp
from jax import lax
from jax.experimental import pallas as pl
from jax.experimental.pallas import tpu as pltpu
from jax.sharding import PartitionSpec as P

AGG = 8
KC = 6
LO = 2
UNROLL = 32
MESH = pl.DeviceIdType.MESH
F32 = jnp.float32
BF16 = jnp.bfloat16


def within(at, size):
    return jnp.minimum(jnp.maximum(at, 0), size - 1)


def make_plan(rows_group, cols_group, dev_rows, small, count_v, plan_v):
    slots, width = small.shape[2], plan_v.shape[1]
    cb, sb, db = (n.bit_length() - 1 for n in (cols_group, slots, dev_rows))
    rows, cols = small[0], small[1]
    lane = lax.broadcasted_iota(jnp.int32, (1, slots), 1)
    key = jnp.where(lane < count_v[...], rows, rows_group)
    across = jnp.broadcast_to(((((key << sb) | lane) << cb) | cols), (slots, slots))
    side = lax.broadcasted_iota(jnp.int32, (slots, slots), 0)
    place = lax.broadcasted_iota(jnp.int32, (slots, slots), 1)
    down = jnp.sum(jnp.where(side == place, across, 0), axis=1, keepdims=True)
    rank = jnp.sum(jnp.where(across < down, 1, 0), axis=1, keepdims=True)
    word = jnp.sum(jnp.where(rank == place, down, 0), axis=0, keepdims=True)
    slot = (word >> cb) & (slots - 1)
    top = word >> (cb + sb)
    same = (top == pltpu.roll(top, 1, 1)) & (lane > 0)
    target = lax.broadcasted_iota(jnp.int32, (slots, width), 1)
    tops = down >> (cb + sb)
    upto = jnp.sum(jnp.where(tops <= target, 1, 0), axis=0, keepdims=True)
    before = jnp.sum(jnp.where(tops < target, 1, 0), axis=0, keepdims=True)
    last = jnp.where(upto > before, upto - 1, slots)
    plan_v[...] = jnp.zeros_like(plan_v)
    right = 2 * (word & (cols_group - 1)) + (slot & 1)
    plan_v[0:1, :slots] = (slot >> 1) | (same.astype(jnp.int32) << 15) | (right << 16)
    plan_v[3:4, :] = last
    plan_v[4:5, :slots] = rows >> db
    plan_v[5:6, :slots] = rows & (dev_rows - 1)
    plan_v[6:7, :slots] = small[2]


def kernel(
    n_row, n_col, a_hbm, p_hbm, rows_hbm, cols_hbm, count_hbm, kslot_hbm, agg_hbm, out_ref,
    small, count_v, agg_v, plan_v, plan_s, ag_ref, in_sem, plan_sem, a_v, pan, agp, colp, pz, ps, q_ref, snd, rcv,
    a_sem, p_send, p_recv, g_send, g_recv, c_send, c_recv, x_send, x_recv,
):
    bw = p_hbm.shape[0]
    dev_rows = ag_ref.shape[0]
    rows_group = n_col * dev_rows
    slots = ps.shape[0] - 1
    ratio = n_col // n_row
    per = n_col // ratio
    owners = per * dev_rows // AGG
    hi = n_col // LO
    row = lax.axis_index("row")
    me = lax.axis_index("col")
    z, x = me // LO, lax.rem(me, LO)
    is_root = row == me // ratio
    part = lax.rem(me, ratio)

    def col_of(d):
        return lax.rem(me + d, n_col)

    barrier = pltpu.get_barrier_semaphore()
    for d in range(1, n_col):
        pl.semaphore_signal(barrier, inc=1, device_id=(row, col_of(d)), device_id_type=MESH)
    for d in range(1, n_row):
        pl.semaphore_signal(
            barrier, inc=1, device_id=(lax.rem(row + d, n_row), me), device_id_type=MESH
        )
    p_ref = pan.at[me]
    loads = [
        pltpu.make_async_copy(src, dst, in_sem.at[i])
        for i, (src, dst) in enumerate(
            [
                (p_hbm, p_ref),
                (rows_hbm, small.at[0]),
                (cols_hbm, small.at[1]),
                (kslot_hbm, small.at[2]),
                (count_hbm, count_v),
                (agg_hbm, agg_v),
            ]
        )
    ]
    for c in loads:
        c.start()

    for c in loads:
        c.wait()
    square = (dev_rows, dev_rows)
    eye = lax.broadcasted_iota(jnp.int32, square, 0) == lax.broadcasted_iota(jnp.int32, square, 1)
    mine = jnp.where(eye, jnp.broadcast_to(agg_v[...].astype(F32), square), 0.0)
    mine = jnp.broadcast_to(jnp.sum(mine, axis=1, keepdims=True), ag_ref.shape)
    ag_ref[...] = mine
    agp[me] = mine
    make_plan(rows_group, n_col // (n_col // n_row) * dev_rows, dev_rows, small, count_v, plan_v)
    pl.semaphore_wait(barrier, n_col + n_row - 2)

    def remote(src, dst, s, r, dev):
        return pltpu.make_async_remote_copy(
            src_ref=src, dst_ref=dst, send_sem=s, recv_sem=r, device_id=dev, device_id_type=MESH
        )

    own = []
    for d in range(1, hi):
        to = lax.rem(z + d, hi) * LO + x
        own.append(remote(p_ref, pan.at[me], p_send.at[len(own)], p_recv.at[me], (row, to)))
    partner = z * LO + (1 - x)
    own.append(remote(p_ref, pan.at[me], p_send.at[len(own)], p_recv.at[me], (row, partner)))
    for c in own:
        c.start()

    def panel_copies(q, src):
        m = lax.rem(q, per)
        return [
            remote(
                src, colp.at[m], c_send.at[m, d - 1], c_recv.at[m],
                (lax.rem(row + d, n_row), me),
            )
            for d in range(1, n_row)
        ]

    def hand_on(q, src):
        @pl.when(is_root & (q // per == part))
        def _():
            for c in panel_copies(q, src):
                c.start()

    plan_copy = pltpu.make_async_copy(plan_v, plan_s, plan_sem)
    plan_copy.start()
    hand_on(me, p_ref)
    marks = [
        remote(ag_ref, agp.at[me], g_send.at[d - 1], g_recv.at[me], (row, col_of(d)))
        for d in range(1, n_col)
    ]
    for c in marks:
        c.start()

    @pl.loop(0, slots // 16)
    def _(g):
        for u in range(8):
            i = g * 8 + u
            lanes = pl.ds(pl.multiple_of(i * (2 * bw), 2 * bw), 2 * bw)
            pltpu.make_async_copy(a_hbm.at[:, lanes], a_v.at[i], a_sem).start()

    pz[...] = jnp.zeros_like(pz)
    ps[slots] = jnp.zeros((bw, bw), BF16)
    q_ref[...] = jnp.zeros_like(q_ref)

    def landed(q):
        remote(p_ref, pan.at[q], p_send.at[0], p_recv.at[q], (row, partner)).wait_recv()

    passed = []
    landed(partner)
    hand_on(partner, pan.at[partner])
    for d in range(1, hi):
        q = lax.rem(z + hi - d, hi) * LO + x
        landed(q)
        c = remote(
            pan.at[q], pan.at[q], p_send.at[hi - 1 + d], p_recv.at[q], (row, partner)
        )
        c.start()
        passed.append(c)
        hand_on(q, pan.at[q])
    for d in range(1, hi):
        q = lax.rem(z + hi - d, hi) * LO + (1 - x)
        landed(q)
        hand_on(q, pan.at[q])

    for m in range(per):
        @pl.when(is_root)
        def _():
            colp[m] = pan[part * per + m]

        @pl.when(jnp.logical_not(is_root))
        def _():
            remote(
                p_ref, colp.at[m], c_send.at[m, 0], c_recv.at[m], (row, partner)
            ).wait_recv()

        for b in range(dev_rows):
            block = colp[m, :, b * bw:(b + 1) * bw]
            pz[2 * (m * dev_rows + b), 0:bw, :] = block
            pz[2 * (m * dev_rows + b) + 1, bw:2 * bw, :] = block
    pltpu.make_async_copy(a_v, a_v, a_sem).wait()

    plan_copy.wait()

    def steps(it, acc):
        for u in range(UNROLL):
            at = it * UNROLL + u
            word = plan_s[0, at]
            left = a_v[word & (slots // 2 - 1)]
            right = pz[(word >> 16) & (pz.shape[0] - 1)]
            keep = ((word >> 15) & 1).astype(F32)
            prod = jnp.dot(left, right, preferred_element_type=F32)
            acc = acc * keep + prod
            ps[at] = acc.astype(BF16)
        return acc

    lax.fori_loop(0, slots // UNROLL, steps, jnp.zeros((bw, bw), F32))

    for d in range(1, n_col):
        q = col_of(d)
        remote(ag_ref, agp.at[q], g_send.at[0], g_recv.at[q], (row, partner)).wait_recv()

    lane = lax.broadcasted_iota(jnp.int32, (1, 2 * bw), 1)

    def fold(c):
        group = c // per
        base = (group * owners).astype(F32)
        total = jnp.zeros((owners * bw, bw), F32)
        for h in range(dev_rows // 4):
            wide = []
            for e in range(2):
                b = 4 * h + 2 * e
                flip = pan[c, :, b * bw:(b + 2) * bw].T
                pair = jnp.concatenate([flip[:bw], flip[bw:]], axis=1)
                mark = jnp.where(lane < bw, agp[c, b:b + 1, :], agp[c, b + 1:b + 2, :]) - base
                wide.append(
                    jnp.concatenate(
                        [pair * jnp.where(mark == o, 1.0, 0.0).astype(BF16) for o in range(owners)],
                        axis=0,
                    )
                )
            right = jnp.concatenate(
                [ps[within(plan_s[3, c * dev_rows + 4 * h + e], slots + 1)] for e in range(4)], axis=0
            )
            total += jnp.dot(
                jnp.concatenate(wide, axis=1), right, preferred_element_type=F32
            )
        return total

    def fold_two(i, carry):
        q_ref[2 * i // per] += fold(2 * i) + fold(2 * i + 1)
        return carry

    lax.fori_loop(0, n_col // 2, fold_two, 0)

    half = bw // 2
    for o in range(n_col):
        g, w = o // owners, o % owners
        even = q_ref[g, pl.ds(w * bw, half, stride=2), :]
        odd = q_ref[g, pl.ds(w * bw + 1, half, stride=2), :]
        snd[o] = jnp.concatenate([even, odd], axis=1).astype(BF16)
    terms = []
    for d in range(1, n_col):
        to = col_of(d)
        terms.append(remote(snd.at[to], rcv.at[me], x_send.at[d - 1], x_recv.at[me], (row, to)))
    for c in terms:
        c.start()
    rcv[me] = snd[me]

    there = lax.broadcasted_iota(jnp.int32, (dev_rows, 2 * bw), 0) == plan_s[5, 0]
    spot = jnp.sum(jnp.where(there, agp[within(plan_s[4, 0], n_col)], 0.0), axis=0, keepdims=True)
    spot = spot.astype(jnp.int32) * KC + plan_s[6, 0]
    for d in range(1, n_col):
        q = col_of(d)
        remote(snd.at[0], rcv.at[q], x_send.at[0], x_recv.at[q], (row, partner)).wait_recv()
    sums = [jnp.zeros((half, 2 * bw), F32) for _ in range(KC)]
    for c in range(n_col):
        value = rcv[c].astype(F32)
        where = (spot + (c - (KC + 1) * me + 8 * n_col * n_col)) & (n_col - 1)
        for k in range(KC):
            sums[k] += jnp.where(where == k, value, 0.0)
    for k in range(KC):
        out_ref[k * half:(k + 1) * half, :] = sums[k].astype(BF16)

    for c in own + passed + marks + terms:
        c.wait_send()
    for m in range(per):
        @pl.when(is_root)
        def _():
            for c in panel_copies(m, pan.at[0]):
                c.wait_send()


def on_device(n_row, n_col, a_vals, p_vals, a_rows, a_cols, a_count, c_slot, agg):
    bw = p_vals.shape[0]
    dev_rows = agg.shape[0]
    slots = a_rows.shape[1]
    rows_group = dev_rows * n_col
    ratio = n_col // n_row
    cols_group = rows_group // ratio
    per = n_col // ratio
    assert rows_group // AGG == n_col and n_col >= KC
    assert all(n & (n - 1) == 0 for n in (n_col, slots, cols_group, dev_rows))
    keep = pl.BlockSpec(memory_space=pltpu.HBM)
    vmem = pl.BlockSpec(memory_space=pltpu.VMEM)
    dma = pltpu.SemaphoreType.DMA
    owners = per * dev_rows // AGG
    out = pl.pallas_call(
        functools.partial(kernel, n_row, n_col),
        out_shape=jax.ShapeDtypeStruct((KC * bw // 2, 2 * bw), BF16),
        in_specs=[keep] * 7,
        out_specs=vmem,
        scratch_shapes=[
            pltpu.VMEM((3, 1, slots), jnp.int32),
            pltpu.VMEM((1, 1), jnp.int32),
            pltpu.VMEM((1, dev_rows), jnp.int32),
            pltpu.VMEM((8, max(slots, rows_group)), jnp.int32),
            pltpu.SMEM((8, max(slots, rows_group)), jnp.int32),
            pltpu.VMEM((dev_rows, 2 * bw), F32),
            dma((6,)), dma,
            pltpu.VMEM((slots // 2, bw, 2 * bw), BF16),
            pltpu.VMEM((n_col, bw, dev_rows * bw), BF16),
            pltpu.VMEM((n_col, dev_rows, 2 * bw), F32),
            pltpu.VMEM((per, bw, dev_rows * bw), BF16),
            pltpu.VMEM((2 * cols_group, 2 * bw, bw), BF16),
            pltpu.VMEM((slots + 1, bw, bw), BF16),
            pltpu.VMEM((ratio, owners * bw, bw), F32),
            pltpu.VMEM((n_col, bw // 2, 2 * bw), BF16),
            pltpu.VMEM((n_col, bw // 2, 2 * bw), BF16),
            dma,
            dma((n_col,)), dma((n_col,)),
            dma((n_col,)), dma((n_col,)),
            dma((per, n_row)), dma((per,)),
            dma((n_col,)), dma((n_col,)),
        ],
        compiler_params=pltpu.CompilerParams(
            collective_id=0, has_side_effects=True, vmem_limit_bytes=67043328
        ),
    )(a_vals, p_vals, a_rows, a_cols, a_count, c_slot, agg.reshape(1, dev_rows))
    return out.astype(F32).reshape(1, KC * bw * bw)


def solution(mesh):
    return jax.shard_map(
        functools.partial(on_device, mesh.shape["row"], mesh.shape["col"]),
        mesh=mesh,
        in_specs=(
            P("row", "col"),
            P(None, ("row", "col")),
            P("row", "col"),
            P("row", "col"),
            P("row", "col"),
            P("row", "col"),
            P(("row", "col")),
        ),
        out_specs=P(("row", "col"), None),
        check_vma=False,
    )
```

```python
import functools

import jax
import jax.numpy as jnp
from jax import lax
from jax.experimental import pallas as pl
from jax.experimental.pallas import tpu as pltpu
from jax.sharding import PartitionSpec as P

AGG = 8
KC = 6
LO = 2
UNROLL = 32
MESH = pl.DeviceIdType.MESH
F32 = jnp.float32
BF16 = jnp.bfloat16


def within(at, size):
    return jnp.minimum(jnp.maximum(at, 0), size - 1)


def make_plan(rows_group, cols_group, dev_rows, small, count_v, plan_v):
    slots, width = small.shape[2], plan_v.shape[1]
    cb, sb, db = (n.bit_length() - 1 for n in (cols_group, slots, dev_rows))
    rows, cols = small[0], small[1]
    lane = lax.broadcasted_iota(jnp.int32, (1, slots), 1)
    key = jnp.where(lane < count_v[...], rows, rows_group)
    across = jnp.broadcast_to(((((key << sb) | lane) << cb) | cols), (slots, slots))
    side = lax.broadcasted_iota(jnp.int32, (slots, slots), 0)
    place = lax.broadcasted_iota(jnp.int32, (slots, slots), 1)
    down = jnp.sum(jnp.where(side == place, across, 0), axis=1, keepdims=True)
    rank = jnp.sum(jnp.where(across < down, 1, 0), axis=1, keepdims=True)
    word = jnp.sum(jnp.where(rank == place, down, 0), axis=0, keepdims=True)
    slot = (word >> cb) & (slots - 1)
    top = word >> (cb + sb)
    same = (top == pltpu.roll(top, 1, 1)) & (lane > 0)
    target = lax.broadcasted_iota(jnp.int32, (slots, width), 1)
    tops = down >> (cb + sb)
    upto = jnp.sum(jnp.where(tops <= target, 1, 0), axis=0, keepdims=True)
    before = jnp.sum(jnp.where(tops < target, 1, 0), axis=0, keepdims=True)
    last = jnp.where(upto > before, upto - 1, slots)
    plan_v[...] = jnp.zeros_like(plan_v)
    right = 2 * (word & (cols_group - 1)) + (slot & 1)
    plan_v[0:1, :slots] = (slot >> 1) | (same.astype(jnp.int32) << 15) | (right << 16)
    plan_v[3:4, :] = last
    plan_v[4:5, :slots] = rows >> db
    plan_v[5:6, :slots] = rows & (dev_rows - 1)
    plan_v[6:7, :slots] = small[2]


def kernel(
    n_row, n_col, a_hbm, p_hbm, rows_hbm, cols_hbm, count_hbm, kslot_hbm, agg_hbm, out_ref,
    small, count_v, agg_v, plan_v, plan_s, ag_ref, in_sem, plan_sem, a_v, pan, agp, colp, pz, ps, q_ref, snd, rcv,
    a_sem, p_send, p_recv, g_send, g_recv, c_send, c_recv, x_send, x_recv,
):
    bw = p_hbm.shape[0]
    dev_rows = ag_ref.shape[0]
    rows_group = n_col * dev_rows
    slots = ps.shape[0] - 1
    ratio = n_col // n_row
    per = n_col // ratio
    owners = per * dev_rows // AGG
    hi = n_col // LO
    row = lax.axis_index("row")
    me = lax.axis_index("col")
    z, x = me // LO, lax.rem(me, LO)
    is_root = row == me // ratio
    part = lax.rem(me, ratio)

    def col_of(d):
        return lax.rem(me + d, n_col)

    barrier = pltpu.get_barrier_semaphore()
    for d in range(1, n_col):
        pl.semaphore_signal(barrier, inc=1, device_id=(row, col_of(d)), device_id_type=MESH)
    for d in range(1, n_row):
        pl.semaphore_signal(
            barrier, inc=1, device_id=(lax.rem(row + d, n_row), me), device_id_type=MESH
        )
    p_ref = pan.at[me]
    loads = [
        pltpu.make_async_copy(src, dst, in_sem.at[i])
        for i, (src, dst) in enumerate(
            [
                (p_hbm, p_ref),
                (rows_hbm, small.at[0]),
                (cols_hbm, small.at[1]),
                (kslot_hbm, small.at[2]),
                (count_hbm, count_v),
                (agg_hbm, agg_v),
            ]
        )
    ]
    for c in loads:
        c.start()

    for c in loads:
        c.wait()
    square = (dev_rows, dev_rows)
    eye = lax.broadcasted_iota(jnp.int32, square, 0) == lax.broadcasted_iota(jnp.int32, square, 1)
    mine = jnp.where(eye, jnp.broadcast_to(agg_v[...].astype(F32), square), 0.0)
    mine = jnp.broadcast_to(jnp.sum(mine, axis=1, keepdims=True), ag_ref.shape)
    ag_ref[...] = mine
    agp[me] = mine
    make_plan(rows_group, n_col // (n_col // n_row) * dev_rows, dev_rows, small, count_v, plan_v)
    pl.semaphore_wait(barrier, n_col + n_row - 2)

    def remote(src, dst, s, r, dev):
        return pltpu.make_async_remote_copy(
            src_ref=src, dst_ref=dst, send_sem=s, recv_sem=r, device_id=dev, device_id_type=MESH
        )

    own = []
    for d in range(1, hi):
        to = lax.rem(z + d, hi) * LO + x
        own.append(remote(p_ref, pan.at[me], p_send.at[len(own)], p_recv.at[me], (row, to)))
    partner = z * LO + (1 - x)
    own.append(remote(p_ref, pan.at[me], p_send.at[len(own)], p_recv.at[me], (row, partner)))
    for c in own:
        c.start()

    def panel_copies(q, src):
        m = lax.rem(q, per)
        return [
            remote(
                src, colp.at[m], c_send.at[m, d - 1], c_recv.at[m],
                (lax.rem(row + d, n_row), me),
            )
            for d in range(1, n_row)
        ]

    def hand_on(q, src):
        @pl.when(is_root & (q // per == part))
        def _():
            for c in panel_copies(q, src):
                c.start()

    plan_copy = pltpu.make_async_copy(plan_v, plan_s, plan_sem)
    plan_copy.start()
    hand_on(me, p_ref)
    marks = [
        remote(ag_ref, agp.at[me], g_send.at[d - 1], g_recv.at[me], (row, col_of(d)))
        for d in range(1, n_col)
    ]
    for c in marks:
        c.start()

    @pl.loop(0, slots // 16)
    def _(g):
        for u in range(8):
            i = g * 8 + u
            lanes = pl.ds(pl.multiple_of(i * (2 * bw), 2 * bw), 2 * bw)
            pltpu.make_async_copy(a_hbm.at[:, lanes], a_v.at[i], a_sem).start()

    pz[...] = jnp.zeros_like(pz)
    ps[slots] = jnp.zeros((bw, bw), BF16)
    q_ref[...] = jnp.zeros_like(q_ref)

    def landed(q):
        remote(p_ref, pan.at[q], p_send.at[0], p_recv.at[q], (row, partner)).wait_recv()

    passed = []
    landed(partner)
    hand_on(partner, pan.at[partner])
    for d in range(1, hi):
        q = lax.rem(z + hi - d, hi) * LO + x
        landed(q)
        c = remote(
            pan.at[q], pan.at[q], p_send.at[hi - 1 + d], p_recv.at[q], (row, partner)
        )
        c.start()
        passed.append(c)
        hand_on(q, pan.at[q])
    for d in range(1, hi):
        q = lax.rem(z + hi - d, hi) * LO + (1 - x)
        landed(q)
        hand_on(q, pan.at[q])

    for m in range(per):
        @pl.when(is_root)
        def _():
            colp[m] = pan[part * per + m]

        @pl.when(jnp.logical_not(is_root))
        def _():
            remote(
                p_ref, colp.at[m], c_send.at[m, 0], c_recv.at[m], (row, partner)
            ).wait_recv()

        for b in range(dev_rows):
            block = colp[m, :, b * bw:(b + 1) * bw]
            pz[2 * (m * dev_rows + b), 0:bw, :] = block
            pz[2 * (m * dev_rows + b) + 1, bw:2 * bw, :] = block
    pltpu.make_async_copy(a_v, a_v, a_sem).wait()

    plan_copy.wait()

    def steps(it, acc):
        for u in range(UNROLL):
            at = it * UNROLL + u
            word = plan_s[0, at]
            left = a_v[word & (slots // 2 - 1)]
            right = pz[(word >> 16) & (pz.shape[0] - 1)]
            keep = ((word >> 15) & 1).astype(F32)
            prod = jnp.dot(left, right, preferred_element_type=F32)
            acc = acc * keep + prod
            ps[at] = acc.astype(BF16)
        return acc

    lax.fori_loop(0, slots // UNROLL, steps, jnp.zeros((bw, bw), F32))

    for d in range(1, n_col):
        q = col_of(d)
        remote(ag_ref, agp.at[q], g_send.at[0], g_recv.at[q], (row, partner)).wait_recv()

    lane = lax.broadcasted_iota(jnp.int32, (1, 2 * bw), 1)

    def fold(c):
        group = c // per
        base = (group * owners).astype(F32)
        total = jnp.zeros((owners * bw, bw), F32)
        for h in range(dev_rows // 4):
            wide = []
            for e in range(2):
                b = 4 * h + 2 * e
                flip = pan[c, :, b * bw:(b + 2) * bw].T
                pair = jnp.concatenate([flip[:bw], flip[bw:]], axis=1)
                mark = jnp.where(lane < bw, agp[c, b:b + 1, :], agp[c, b + 1:b + 2, :]) - base
                wide.append(
                    jnp.concatenate(
                        [pair * jnp.where(mark == o, 1.0, 0.0).astype(BF16) for o in range(owners)],
                        axis=0,
                    )
                )
            right = jnp.concatenate(
                [ps[within(plan_s[3, c * dev_rows + 4 * h + e], slots + 1)] for e in range(4)], axis=0
            )
            total += jnp.dot(
                jnp.concatenate(wide, axis=1), right, preferred_element_type=F32
            )
        return total

    def fold_two(i, carry):
        q_ref[2 * i // per] += fold(2 * i) + fold(2 * i + 1)
        return carry

    half = bw // 2

    def term(o):
        return remote(snd.at[o], rcv.at[me], x_send.at[o], x_recv.at[me], (row, o))

    for g in range(ratio):
        lax.fori_loop(g * per // 2, (g + 1) * per // 2, fold_two, 0)
        for w in range(owners):
            o = g * owners + w
            even = q_ref[g, pl.ds(w * bw, half, stride=2), :]
            odd = q_ref[g, pl.ds(w * bw + 1, half, stride=2), :]
            snd[o] = jnp.concatenate([even, odd], axis=1).astype(BF16)
        for w in range(owners):
            o = g * owners + w

            @pl.when(me != o)
            def _():
                term(o).start()

    rcv[me] = snd[me]

    there = lax.broadcasted_iota(jnp.int32, (dev_rows, 2 * bw), 0) == plan_s[5, 0]
    spot = jnp.sum(jnp.where(there, agp[within(plan_s[4, 0], n_col)], 0.0), axis=0, keepdims=True)
    spot = spot.astype(jnp.int32) * KC + plan_s[6, 0]
    for d in range(1, n_col):
        q = col_of(d)
        remote(snd.at[0], rcv.at[q], x_send.at[0], x_recv.at[q], (row, partner)).wait_recv()
    sums = [jnp.zeros((half, 2 * bw), F32) for _ in range(KC)]
    for c in range(n_col):
        value = rcv[c].astype(F32)
        where = (spot + (c - (KC + 1) * me + 8 * n_col * n_col)) & (n_col - 1)
        for k in range(KC):
            sums[k] += jnp.where(where == k, value, 0.0)
    for k in range(KC):
        out_ref[k * half:(k + 1) * half, :] = sums[k].astype(BF16)

    for c in own + passed + marks:
        c.wait_send()
    for o in range(n_col):
        @pl.when(me != o)
        def _():
            term(o).wait_send()

    for m in range(per):
        @pl.when(is_root)
        def _():
            for c in panel_copies(m, pan.at[0]):
                c.wait_send()


def on_device(n_row, n_col, a_vals, p_vals, a_rows, a_cols, a_count, c_slot, agg):
    bw = p_vals.shape[0]
    dev_rows = agg.shape[0]
    slots = a_rows.shape[1]
    rows_group = dev_rows * n_col
    ratio = n_col // n_row
    cols_group = rows_group // ratio
    per = n_col // ratio
    assert rows_group // AGG == n_col and n_col >= KC
    assert all(n & (n - 1) == 0 for n in (n_col, slots, cols_group, dev_rows))
    keep = pl.BlockSpec(memory_space=pltpu.HBM)
    vmem = pl.BlockSpec(memory_space=pltpu.VMEM)
    dma = pltpu.SemaphoreType.DMA
    owners = per * dev_rows // AGG
    out = pl.pallas_call(
        functools.partial(kernel, n_row, n_col),
        out_shape=jax.ShapeDtypeStruct((KC * bw // 2, 2 * bw), BF16),
        in_specs=[keep] * 7,
        out_specs=vmem,
        scratch_shapes=[
            pltpu.VMEM((3, 1, slots), jnp.int32),
            pltpu.VMEM((1, 1), jnp.int32),
            pltpu.VMEM((1, dev_rows), jnp.int32),
            pltpu.VMEM((8, max(slots, rows_group)), jnp.int32),
            pltpu.SMEM((8, max(slots, rows_group)), jnp.int32),
            pltpu.VMEM((dev_rows, 2 * bw), F32),
            dma((6,)), dma,
            pltpu.VMEM((slots // 2, bw, 2 * bw), BF16),
            pltpu.VMEM((n_col, bw, dev_rows * bw), BF16),
            pltpu.VMEM((n_col, dev_rows, 2 * bw), F32),
            pltpu.VMEM((per, bw, dev_rows * bw), BF16),
            pltpu.VMEM((2 * cols_group, 2 * bw, bw), BF16),
            pltpu.VMEM((slots + 1, bw, bw), BF16),
            pltpu.VMEM((ratio, owners * bw, bw), F32),
            pltpu.VMEM((n_col, bw // 2, 2 * bw), BF16),
            pltpu.VMEM((n_col, bw // 2, 2 * bw), BF16),
            dma,
            dma((n_col,)), dma((n_col,)),
            dma((n_col,)), dma((n_col,)),
            dma((per, n_row)), dma((per,)),
            dma((n_col,)), dma((n_col,)),
        ],
        compiler_params=pltpu.CompilerParams(
            collective_id=0, has_side_effects=True, vmem_limit_bytes=67043328
        ),
    )(a_vals, p_vals, a_rows, a_cols, a_count, c_slot, agg.reshape(1, dev_rows))
    return out.astype(F32).reshape(1, KC * bw * bw)


def solution(mesh):
    return jax.shard_map(
        functools.partial(on_device, mesh.shape["row"], mesh.shape["col"]),
        mesh=mesh,
        in_specs=(
            P("row", "col"),
            P(None, ("row", "col")),
            P("row", "col"),
            P("row", "col"),
            P("row", "col"),
            P("row", "col"),
            P(("row", "col")),
        ),
        out_specs=P(("row", "col"), None),
        check_vma=False,
    )
```
